32 devices in a mesh: groups: 2 (over y), gx: 4 (over z), gy: 2 (over x), gz: 2 (over core).
Axes of the slice: x: 2, y: 2, z: 4, core: 2. Of those that a mesh axis runs over, the one named last changes fastest.
Arguments:
- polar_angle: float32 [16, 512, 256], P('gz', ('groups', 'gx'), 'gy'), parts along dimension 1, may hold values from -3.140625 to 3.140625
- azimuth: float32 [16, 512, 256], P('gz', ('groups', 'gx'), 'gy'), parts along dimension 1, may hold values from -3.140625 to 3.140625
- classes: int32 [6, 16, 512, 256], P(None, 'gz', ('groups', 'gx'), 'gy'), parts along dimension 2, may hold values from 0 to 7, as said below
- exchange_table: float32 [8], replicated, may hold values from 0.3 to 1.5
Outputs:
- spins_final: float32 [3, 16, 512, 256], P(None, 'gz', ('groups', 'gx'), 'gy'), parts along dimension 2
- modes_mid: float32 [32, 6144], P(('groups', 'gx')), parts along dimension 0
- modes_end: float32 [32, 6144], P(('groups', 'gx')), parts along dimension 0
The draws below stay inside these ranges and needn't reach their ends.
There are 2 independent parts, one for each index of `groups`. The reference program is written for one: setup_inputs(seed, part) draws one part's arguments, and reference() takes and returns one part's arrays. A program takes and returns all parts, laid end to end along the dimension named above; an argument that names none is the same for every part. Nothing has to cross between parts.
Inputs may be any that keep to these rules, and one draw needn't show every extreme that they name: `classes`: entry 3 + d of a site equals entry d of its lower neighbour along direction d (periodically), so every bond has one class seen from both ends.
All inputs are finite; a program needn't handle non-finite values.
Results may differ from the reference program's by a relative error of at most 0.0001.
Values sent between devices are 32-bit elements; how exact they have to be, the bound alone decides.
A program may use at most 128 MiB of HBM per device.

```python
import math
import jax
import jax.numpy as jnp
from jax import lax

KX = 32
KY = 32
NCLASS = 8
STEPS = 4
NX = 256
NY = 256
NZ = 16


def draw_classes(key, part):
    upper = jax.random.randint(key, (3, NZ, NX, NY), 0, NCLASS).astype(jnp.int32)
    lower = jnp.stack([jnp.roll(upper[0], 1, axis=1), jnp.roll(upper[1], 1, axis=2), jnp.roll(upper[2], 1, axis=0)])
    return jnp.concatenate([upper, lower], 0).astype(jnp.int32)


def setup_inputs(seed: int = 0, part: int = 0) -> dict:
    key_list = jax.random.split(jax.random.key(seed), 5)
    part_splits = jax.random.split(jax.random.fold_in(key_list[4], part), 5)
    return {
        "polar_angle": jnp.clip(jax.random.uniform(part_splits[0], (NZ, NX, NY), jnp.float32, -3.140625, 3.140625), -3.140625, 3.140625),
        "azimuth": jnp.clip(jax.random.uniform(part_splits[1], (NZ, NX, NY), jnp.float32, -3.140625, 3.140625), -3.140625, 3.140625),
        "classes": draw_classes(jax.random.fold_in(jax.random.fold_in(key_list[4], part), 71), part),
        "exchange_table": jnp.clip(jax.random.uniform(key_list[3], (NCLASS,), jnp.float32, 0.3, 1.5), 0.3, 1.5),
    }


time_step = 0.1
damping = 0.1


def cross_three(first, second):
    return jnp.stack([first[1] * second[2] - first[2] * second[1],
                      first[2] * second[0] - first[0] * second[2],
                      first[0] * second[1] - first[1] * second[0]])


def velocity(spin_field, coupling, neighbours):
    local_field = coupling[0][None] * neighbours[0]
    for direction in range(1, 6):
        local_field = local_field + coupling[direction][None] * neighbours[direction]
    torque = cross_three(spin_field, local_field)
    return -torque - damping * cross_three(spin_field, torque)


def rolled(spin_field):
    return [jnp.roll(spin_field, -1, 2), jnp.roll(spin_field, -1, 3), jnp.roll(spin_field, -1, 1),
            jnp.roll(spin_field, 1, 2), jnp.roll(spin_field, 1, 3), jnp.roll(spin_field, 1, 1)]


def heun_step(spin_field, coupling):
    slope_first = velocity(spin_field, coupling, rolled(spin_field))
    predicted = spin_field + time_step * slope_first
    slope_second = velocity(predicted, coupling, rolled(predicted))
    return spin_field + (0.5 * time_step) * (slope_first + slope_second)


def phase_table(wave_count, length, total_length):
    position = jnp.arange(length, dtype=jnp.int32)
    numbers = jnp.arange(wave_count, dtype=jnp.int32)
    index = (position[:, None] * numbers[None, :]) % total_length
    phase = index.astype(jnp.float32) * (2.0 * math.pi / total_length)
    return jnp.cos(phase), jnp.sin(phase)


def project(spin_field, x_table, y_table, z_cos, z_sin, scale):
    depth, wide_x, wide_y = spin_field.shape[1:]
    along_y = jnp.dot(spin_field.reshape(-1, wide_y), y_table, precision=lax.Precision.HIGHEST,
                      preferred_element_type=jnp.float32).reshape(3, depth, wide_x, 2 * KY)
    along_x = jnp.einsum('czxk,xm->czmk', along_y, x_table, precision=lax.Precision.HIGHEST)
    even_even = along_x[:, :, :KX, :KY]
    even_odd = along_x[:, :, :KX, KY:]
    odd_even = along_x[:, :, KX:, :KY]
    odd_odd = along_x[:, :, KX:, KY:]
    cosine_part = even_even - odd_odd
    sine_part = odd_even + even_odd
    hp = lax.Precision.HIGHEST
    real_part = jnp.einsum('czab,zk->kcab', cosine_part, z_cos, precision=hp) - jnp.einsum('czab,zk->kcab', sine_part, z_sin, precision=hp)
    imag_part = -(jnp.einsum('czab,zk->kcab', sine_part, z_cos, precision=hp) + jnp.einsum('czab,zk->kcab', cosine_part, z_sin, precision=hp))
    stacked = jnp.stack([real_part, imag_part], 1) * scale
    return stacked.reshape(z_cos.shape[1], -1)


def reference(polar_angle, azimuth, classes, exchange_table):
    spin_field = jnp.stack([jnp.sin(polar_angle) * jnp.cos(azimuth),
                            jnp.sin(polar_angle) * jnp.sin(azimuth),
                            jnp.cos(polar_angle)])
    coupling = jnp.take(exchange_table, classes)
    x_cos, x_sin = phase_table(KX, NX, NX)
    y_cos, y_sin = phase_table(KY, NY, NY)
    z_cos, z_sin = phase_table(NZ, NZ, NZ)
    x_table = jnp.concatenate([x_cos, x_sin], 1)
    y_table = jnp.concatenate([y_cos, y_sin], 1)
    scale = float(NX * NY * NZ) ** -0.5
    modes_mid = None
    for turn_index in range(STEPS):
        spin_field = heun_step(spin_field, coupling)
        if turn_index == 1:
            modes_mid = project(spin_field, x_table, y_table, z_cos, z_sin, scale)
    modes_end = project(spin_field, x_table, y_table, z_cos, z_sin, scale)
    return spin_field, modes_mid, modes_end
```

```python
import functools
import math

import jax
import jax.numpy as jnp
from jax import lax
from jax.experimental import pallas as pl
from jax.experimental.pallas import tpu as pltpu
from jax.sharding import PartitionSpec as P

KX = 32
KY = 32
STEPS = 4
HALO = 8
MESH = pl.DeviceIdType.MESH

time_step = 0.1
damping = 0.1


def sin_cos(angle):
    turns = jnp.floor(angle * (2.0 / math.pi) + 0.5)
    rest = angle - turns * 1.5703125
    rest = rest - turns * 4.837512969970703125e-4
    rest = rest - turns * 7.54978995489188216e-8
    square = rest * rest
    sine = rest + rest * square * (
        -1.6666654611e-1 + square * (8.3321608736e-3 + square * -1.9515295891e-4)
    )
    cosine = (1.0 - 0.5 * square) + square * square * (
        4.166664568298827e-2 + square * (-1.388731625493765e-3 + square * 2.443315711809948e-5)
    )
    size = jnp.abs(turns)
    odd = size == 1.0
    half = size == 2.0
    sine_out = jnp.where(odd, jnp.where(turns > 0.0, cosine, -cosine), jnp.where(half, -sine, sine))
    cosine_out = jnp.where(odd, jnp.where(turns > 0.0, -sine, sine), jnp.where(half, -cosine, cosine))
    return sine_out, cosine_out


def spins_of(polar, azimuth):
    sine_polar, cosine_polar = sin_cos(polar)
    sine_azimuth, cosine_azimuth = sin_cos(azimuth)
    return sine_polar * cosine_azimuth, sine_polar * sine_azimuth, cosine_polar


def lookup(classes, table_ref):
    values = [table_ref[i] for i in range(table_ref.shape[0])]
    bit = 1
    level = None
    while len(values) > 1:
        mask = (classes & bit) != 0
        values = [
            jnp.where(mask, values[i + 1], values[i]) if i + 1 < len(values) else values[i]
            for i in range(0, len(values), 2)
        ]
        bit *= 2
    return values[0] + jnp.zeros(classes.shape, jnp.float32)


def velocity_of(spin, field):
    s0, s1, s2 = spin
    h0, h1, h2 = field
    t0 = s1 * h2 - s2 * h1
    t1 = s2 * h0 - s0 * h2
    t2 = s0 * h1 - s1 * h0
    return (
        -t0 - damping * (s1 * t2 - s2 * t1),
        -t1 - damping * (s2 * t0 - s0 * t2),
        -t2 - damping * (s0 * t1 - s1 * t0),
    )


def evolve_kernel(sizes, polar_ref, azimuth_ref, classes_ref, table_ref, mid_ref, end_ref,
                  S, Q, J, GS, GQ, GJ, OS, OQ, ins, low, high, lowk, highk,
                  pack, left_pack, right_pack,
                  xs, xr, ys, yr, zs, zr, gs, gr, osem):
    nx, ny, nz = sizes
    depth, wide, lanes = polar_ref.shape
    ext = wide + 2 * HALO
    tiles = ext // 8
    inner = wide // 8
    group = 2 * HALO
    me_x, me_y, me_z = lax.axis_index("gx"), lax.axis_index("gy"), lax.axis_index("gz")

    def at(axis, me, n, step):
        return {axis: lax.rem(me + (step + n), n)}

    x_left, x_right = at("gx", me_x, nx, -1), at("gx", me_x, nx, 1)
    y_left, y_right = at("gy", me_y, ny, -1), at("gy", me_y, ny, 1)
    z_down, z_up = at("gz", me_z, nz, -1), at("gz", me_z, nz, 1)

    barrier = pltpu.get_barrier_semaphore()
    for who in (x_left, x_right, y_left, y_right, z_down, z_up):
        pl.semaphore_signal(barrier, inc=1, device_id=who, device_id_type=MESH)
    pl.semaphore_wait(barrier, 6)

    def remote(src, dst, send, recv, who):
        return pltpu.make_async_remote_copy(
            src_ref=src, dst_ref=dst, send_sem=send, recv_sem=recv, device_id=who, device_id_type=MESH
        )

    top = pl.ds(wide - HALO, HALO)
    bottom = pl.ds(0, HALO)
    x_copies = [
        remote(polar_ref.at[:, top, :], low.at[0], xs.at[0], xr.at[0], x_right),
        remote(azimuth_ref.at[:, top, :], low.at[1], xs.at[1], xr.at[1], x_right),
        remote(classes_ref.at[:, :, top, :], lowk, xs.at[2], xr.at[2], x_right),
        remote(polar_ref.at[:, bottom, :], high.at[0], xs.at[3], xr.at[3], x_left),
        remote(azimuth_ref.at[:, bottom, :], high.at[1], xs.at[4], xr.at[4], x_left),
        remote(classes_ref.at[:, :, bottom, :], highk, xs.at[5], xr.at[5], x_left),
    ]
    for copy in x_copies:
        copy.start()

    lane = lax.broadcasted_iota(jnp.int32, (8, lanes), 1)
    group_of = lane // group
    place = lane % group

    def spread(z, polar, azimuth, classes_at, row):
        where_to = pl.ds(row, 8)
        shift = group * z + HALO
        mine = group_of == z
        spin = spins_of(polar, azimuth)
        for c in range(3):
            S[c, z + 1, where_to, :] = spin[c]
            old = pack[c, where_to, :]
            pack[c, where_to, :] = jnp.where(mine, pltpu.roll(spin[c], shift, 1), old)
        for d in range(6):
            value = lookup(classes_at(d), table_ref)
            J[d, z, where_to, :] = value
            old = pack[3 + d, where_to, :]
            pack[3 + d, where_to, :] = jnp.where(mine, pltpu.roll(value, shift, 1), old)

    pack[...] = jnp.zeros(pack.shape, jnp.float32)

    def own(z, carry):
        for r in range(inner):
            rows = pl.ds(8 * r, 8)
            spread(z, polar_ref[z, rows, :], azimuth_ref[z, rows, :],
                   lambda d: classes_ref[d, z, rows, :], HALO + 8 * r)
        return carry

    lax.fori_loop(0, depth, own, 0)

    def y_copies(part):
        rows = (pl.ds(HALO, wide), pl.ds(0, HALO), pl.ds(HALO + wide, HALO))[part]
        made = [remote(pack.at[:, rows, :], left_pack.at[:, rows, :], ys.at[part], yr.at[part], y_right)]
        if ny > 2:
            made.append(remote(pack.at[:, rows, :], right_pack.at[:, rows, :], ys.at[3 + part], yr.at[3 + part], y_left))
        return made

    def z_copies(field, base):
        return [
            remote(field.at[:, 1], field.at[:, depth + 1], zs.at[base], zr.at[base], z_down),
            remote(field.at[:, depth], field.at[:, 0], zs.at[base + 1], zr.at[base + 1], z_up),
        ]

    def g_copy(ghost, other, base):
        return remote(ghost, other, gs.at[base], gr.at[base], z_up)

    for copy in y_copies(0):
        copy.start()
    for copy in x_copies:
        copy.wait()

    def edges(z, carry):
        spread(z, low[0, z], low[1, z], lambda d: lowk[d, z], 0)
        spread(z, high[0, z], high[1, z], lambda d: highk[d, z], HALO + wide)
        return carry

    lax.fori_loop(0, depth, edges, 0)
    for part in (1, 2):
        for copy in y_copies(part):
            copy.start()
    for copy in z_copies(S, 0):
        copy.start()
    for part in range(3):
        for copy in y_copies(part):
            copy.wait()
    from_right = left_pack if ny == 2 else right_pack

    def ghosts(r, carry):
        rows = pl.ds(pl.multiple_of(8 * r, 8), 8)
        for f in range(9):
            value = jnp.where(place < HALO, left_pack[f, rows, :], from_right[f, rows, :])
            if f < 3:
                GS[f, rows, :] = value
            else:
                GJ[f - 3, rows, :] = value
        return carry

    lax.fori_loop(0, tiles, ghosts, 0)
    g_copy(GS, OS, 0).start()

    def x_pair(ref, r, value):
        if r < tiles - 1:
            ahead = ref[pl.ds(8 * r + 1, 8), :]
        else:
            ahead = pltpu.roll(value, 7, 0)
        if r > 0:
            behind = ref[pl.ds(8 * r - 1, 8), :]
        else:
            behind = pltpu.roll(value, 1, 0)
        return ahead, behind

    def plane(F, G, z, finish):
        up_shift = lanes - (group * z + HALO)
        left_mask = lane == group * z + HALO - 1
        right_mask = lane == group * z + HALO
        for r in range(tiles):
            rows = pl.ds(8 * r, 8)
            coupling = [J[d, z, rows, :] for d in range(6)]
            spin, field = [], []
            for c in range(3):
                M = F[c, z + 1, rows, :]
                ahead, behind = x_pair(F.at[c, z + 1], r, M)
                U = pltpu.roll(G[c, rows, :], up_shift, 1)
                right = pltpu.roll(jnp.where(lane == 0, U, M), lanes - 1, 1)
                left = pltpu.roll(jnp.where(lane == lanes - 1, U, M), 1, 1)
                total = coupling[0] * ahead + coupling[1] * right
                total = total + coupling[2] * F[c, z + 2, rows, :]
                total = total + coupling[3] * behind
                total = total + coupling[4] * left
                total = total + coupling[5] * F[c, z, rows, :]
                ins[c, rows, :] = jnp.where(
                    left_mask, pltpu.roll(M, group * z + HALO - 1, 1),
                    jnp.where(right_mask, pltpu.roll(M, group * z + HALO + 1, 1), ins[c, rows, :]))
                spin.append(M)
                field.append(total)
            finish(spin, velocity_of(spin, field), z, rows)

    def ghost_pass(G, other, finish):
        for r in range(tiles):
            rows = pl.ds(8 * r, 8)
            coupling = [GJ[d, rows, :] for d in range(6)]
            spin, field = [], []
            for c in range(3):
                M = G[c, rows, :]
                O = other[c, rows, :]
                I = ins[c, rows, :]
                ahead, behind = x_pair(G.at[c], r, M)
                right = jnp.where(place == HALO - 1, I, pltpu.roll(M, lanes - 1, 1))
                left = jnp.where(place == HALO, I, pltpu.roll(M, 1, 1))
                above = pltpu.roll(jnp.where(lane >= group, M, O), lanes - group, 1)
                below = pltpu.roll(jnp.where(lane < lanes - group, M, O), group, 1)
                total = coupling[0] * ahead + coupling[1] * right
                total = total + coupling[2] * above
                total = total + coupling[3] * behind
                total = total + coupling[4] * left
                total = total + coupling[5] * below
                spin.append(M)
                field.append(total)
            finish(spin, velocity_of(spin, field), rows)

    def predict(spin, speed, z, rows):
        for c in range(3):
            Q[c, z + 1, rows, :] = spin[c] + time_step * speed[c]

    def predict_ghost(spin, speed, rows):
        for c in range(3):
            GQ[c, rows, :] = spin[c] + time_step * speed[c]

    def correct(spin, speed, z, rows):
        for c in range(3):
            S[c, z + 1, rows, :] = 0.5 * (S[c, z + 1, rows, :] + spin[c]) + 0.5 * time_step * speed[c]

    def correct_ghost(spin, speed, rows):
        for c in range(3):
            GS[c, rows, :] = 0.5 * (GS[c, rows, :] + spin[c]) + 0.5 * time_step * speed[c]

    ins[...] = jnp.zeros(ins.shape, jnp.float32)

    def stage(F, G, O, base, finish, finish_ghost, send_main, send_ghost):
        def inside(z, carry):
            plane(F, G, z, finish)
            return carry

        def outside(i, carry):
            plane(F, G, i * (depth - 1), finish)
            return carry

        lax.fori_loop(1, depth - 1, inside, 0)
        for copy in z_copies(F, 2 * base):
            copy.wait()
        lax.fori_loop(0, 2, outside, 0)
        send_main()
        g_copy(G, O, base).wait()
        ghost_pass(G, O, finish_ghost)
        send_ghost()

    def out_copy(target):
        return pltpu.make_async_copy(S.at[:, pl.ds(1, depth), pl.ds(HALO, wide), :], target, osem.at[0])

    def step(turn, carry):
        def send_q():
            for copy in z_copies(Q, 2):
                copy.start()

        def send_s():
            @pl.when(turn < STEPS - 1)
            def _():
                for copy in z_copies(S, 0):
                    copy.start()

        def send_gs():
            @pl.when(turn < STEPS - 1)
            def _():
                g_copy(GS, OS, 0).start()

        stage(S, GS, OS, 0, predict, predict_ghost, send_q, lambda: g_copy(GQ, OQ, 1).start())

        @pl.when(turn == 2)
        def _():
            out_copy(mid_ref).wait()

        stage(Q, GQ, OQ, 1, correct, correct_ghost, send_s, send_gs)

        @pl.when(turn == 1)
        def _():
            out_copy(mid_ref).start()

        return carry

    lax.fori_loop(0, STEPS, step, 0)
    out_copy(end_ref).start()
    out_copy(end_ref).wait()


def evolve(polar_angle, azimuth, classes, exchange_table):
    depth, wide, lanes = polar_angle.shape
    sizes = (lax.axis_size("gx"), lax.axis_size("gy"), lax.axis_size("gz"))
    assert sizes[2] == 2 and depth * 2 * HALO == lanes
    ext = wide + 2 * HALO
    f32 = jnp.float32
    out = jax.ShapeDtypeStruct((3, depth, wide, lanes), f32)
    vmem = pl.BlockSpec(memory_space=pltpu.VMEM)
    anywhere = pl.BlockSpec(memory_space=pl.ANY)
    V = pltpu.VMEM
    D = pltpu.SemaphoreType.DMA
    return pl.pallas_call(
        functools.partial(evolve_kernel, sizes),
        out_shape=(out, out),
        in_specs=[vmem, vmem, vmem, pl.BlockSpec(memory_space=pltpu.SMEM)],
        out_specs=(anywhere, anywhere),
        scratch_shapes=[
            V((3, depth + 2, ext, lanes), f32), V((3, depth + 2, ext, lanes), f32),
            V((6, depth, ext, lanes), f32),
            V((3, ext, lanes), f32), V((3, ext, lanes), f32), V((6, ext, lanes), f32),
            V((3, ext, lanes), f32), V((3, ext, lanes), f32), V((3, ext, lanes), f32),
            V((2, depth, HALO, lanes), f32), V((2, depth, HALO, lanes), f32),
            V((6, depth, HALO, lanes), jnp.int32), V((6, depth, HALO, lanes), jnp.int32),
            V((9, ext, lanes), f32), V((9, ext, lanes), f32), V((9, ext, lanes), f32),
            D((6,)), D((6,)), D((6,)), D((6,)), D((4,)), D((4,)), D((2,)), D((2,)), D((1,)),
        ],
        compiler_params=pltpu.CompilerParams(collective_id=0, has_side_effects=True, vmem_limit_bytes=48 * 1024 * 1024),
        name="evolve",
    )(polar_angle, azimuth, classes, exchange_table)


def phase_table(wave_count, length, total_length, offset):
    position = jnp.arange(length, dtype=jnp.int32) + offset
    numbers = jnp.arange(wave_count, dtype=jnp.int32)
    index = position[:, None] * numbers[None, :] % total_length
    phase = index.astype(jnp.float32) * (2.0 * math.pi / total_length)
    return (jnp.cos(phase), jnp.sin(phase))


def project(spin_field, x_table, y_table, z_cos, z_sin, scale):
    depth, wide_x, wide_y = spin_field.shape[1:]
    along_y = jnp.dot(
        spin_field.reshape(-1, wide_y),
        y_table,
        precision=lax.Precision.HIGHEST,
        preferred_element_type=jnp.float32,
    ).reshape(3, depth, wide_x, 2 * KY)
    along_x = jnp.einsum("czxk,xm->czmk", along_y, x_table, precision=lax.Precision.HIGHEST)
    even_even = along_x[:, :, :KX, :KY]
    even_odd = along_x[:, :, :KX, KY:]
    odd_even = along_x[:, :, KX:, :KY]
    odd_odd = along_x[:, :, KX:, KY:]
    cosine_part = even_even - odd_odd
    sine_part = odd_even + even_odd
    hp = lax.Precision.HIGHEST
    real_part = jnp.einsum("czab,zk->kcab", cosine_part, z_cos, precision=hp) - jnp.einsum(
        "czab,zk->kcab", sine_part, z_sin, precision=hp
    )
    imag_part = -(
        jnp.einsum("czab,zk->kcab", sine_part, z_cos, precision=hp)
        + jnp.einsum("czab,zk->kcab", cosine_part, z_sin, precision=hp)
    )
    stacked = jnp.stack([real_part, imag_part], 1) * scale
    return stacked.reshape(z_cos.shape[1], -1)


def reduce_modes(partial_value):
    blocks = lax.psum_scatter(partial_value, "gx", scatter_dimension=0, tiled=True)
    return lax.psum(blocks, ("gy", "gz"))


def body(polar_angle, azimuth, classes, exchange_table):
    depth, wide_x, wide_y = polar_angle.shape
    total_x = wide_x * lax.axis_size("gx")
    total_y = wide_y * lax.axis_size("gy")
    total_z = depth * lax.axis_size("gz")
    x_cos, x_sin = phase_table(KX, wide_x, total_x, lax.axis_index("gx") * wide_x)
    y_cos, y_sin = phase_table(KY, wide_y, total_y, lax.axis_index("gy") * wide_y)
    z_cos, z_sin = phase_table(total_z, depth, total_z, lax.axis_index("gz") * depth)
    x_table = jnp.concatenate([x_cos, x_sin], 1)
    y_table = jnp.concatenate([y_cos, y_sin], 1)
    scale = float(total_x * total_y * total_z) ** (-0.5)
    spin_mid, spin_field = evolve(polar_angle, azimuth, classes, exchange_table)
    partial_mid = project(spin_mid, x_table, y_table, z_cos, z_sin, scale)
    partial_end = project(spin_field, x_table, y_table, z_cos, z_sin, scale)
    width = partial_end.shape[1]
    both_modes = reduce_modes(jnp.concatenate([partial_mid, partial_end], 1))
    modes_mid = both_modes[:, :width]
    modes_end = both_modes[:, width:]
    return (spin_field, modes_mid, modes_end)


def solution(mesh):
    return jax.shard_map(
        body,
        mesh=mesh,
        in_specs=(
            P("gz", ("groups", "gx"), "gy"),
            P("gz", ("groups", "gx"), "gy"),
            P(None, "gz", ("groups", "gx"), "gy"),
            P(),
        ),
        out_specs=(
            P(None, "gz", ("groups", "gx"), "gy"),
            P(("groups", "gx"), None),
            P(("groups", "gx"), None),
        ),
        check_vma=False,
    )
```

```python
import functools
import math

import jax
import jax.numpy as jnp
import numpy as np
from jax import lax
from jax.experimental import pallas as pl
from jax.experimental.pallas import tpu as pltpu
from jax.sharding import PartitionSpec as P

KX = 32
KY = 32
STEPS = 4
HALO = 8
MESH = pl.DeviceIdType.MESH

time_step = 0.1
damping = 0.1


def sin_cos(angle):
    turns = jnp.floor(angle * (2.0 / math.pi) + 0.5)
    rest = angle - turns * 1.5703125
    rest = rest - turns * 4.837512969970703125e-4
    rest = rest - turns * 7.54978995489188216e-8
    square = rest * rest
    sine = rest + rest * square * (
        -1.6666654611e-1 + square * (8.3321608736e-3 + square * -1.9515295891e-4)
    )
    cosine = (1.0 - 0.5 * square) + square * square * (
        4.166664568298827e-2 + square * (-1.388731625493765e-3 + square * 2.443315711809948e-5)
    )
    size = jnp.abs(turns)
    odd = size == 1.0
    half = size == 2.0
    sine_out = jnp.where(odd, jnp.where(turns > 0.0, cosine, -cosine), jnp.where(half, -sine, sine))
    cosine_out = jnp.where(odd, jnp.where(turns > 0.0, -sine, sine), jnp.where(half, -cosine, cosine))
    return sine_out, cosine_out


def spins_of(polar, azimuth):
    sine_polar, cosine_polar = sin_cos(polar)
    sine_azimuth, cosine_azimuth = sin_cos(azimuth)
    return sine_polar * cosine_azimuth, sine_polar * sine_azimuth, cosine_polar


def lookup(classes, table_ref):
    values = [table_ref[i] for i in range(table_ref.shape[0])]
    bit = 1
    level = None
    while len(values) > 1:
        mask = (classes & bit) != 0
        values = [
            jnp.where(mask, values[i + 1], values[i]) if i + 1 < len(values) else values[i]
            for i in range(0, len(values), 2)
        ]
        bit *= 2
    return values[0] + jnp.zeros(classes.shape, jnp.float32)


def velocity_of(spin, field):
    s0, s1, s2 = spin
    h0, h1, h2 = field
    t0 = s1 * h2 - s2 * h1
    t1 = s2 * h0 - s0 * h2
    t2 = s0 * h1 - s1 * h0
    return (
        -t0 - damping * (s1 * t2 - s2 * t1),
        -t1 - damping * (s2 * t0 - s0 * t2),
        -t2 - damping * (s0 * t1 - s1 * t0),
    )


def evolve_kernel(sizes, polar_ref, azimuth_ref, classes_ref, table_ref, mid_ref, end_ref,
                  S, Q, J, GS, GQ, GJ, OS, OQ, ins, low, high, lowk, highk,
                  pack, left_pack, right_pack,
                  xs, xr, ys, yr, zs, zr, gs, gr, osem):
    nx, ny, nz = sizes
    depth, wide, lanes = polar_ref.shape
    ext = wide + 2 * HALO
    tiles = ext // 8
    inner = wide // 8
    group = 2 * HALO
    me_x, me_y, me_z = lax.axis_index("gx"), lax.axis_index("gy"), lax.axis_index("gz")

    def at(axis, me, n, step):
        return {axis: lax.rem(me + (step + n), n)}

    x_left, x_right = at("gx", me_x, nx, -1), at("gx", me_x, nx, 1)
    y_left, y_right = at("gy", me_y, ny, -1), at("gy", me_y, ny, 1)
    z_down, z_up = at("gz", me_z, nz, -1), at("gz", me_z, nz, 1)

    barrier = pltpu.get_barrier_semaphore()
    for who in (x_left, x_right, y_left, y_right, z_down, z_up):
        pl.semaphore_signal(barrier, inc=1, device_id=who, device_id_type=MESH)
    pl.semaphore_wait(barrier, 6)

    def remote(src, dst, send, recv, who):
        return pltpu.make_async_remote_copy(
            src_ref=src, dst_ref=dst, send_sem=send, recv_sem=recv, device_id=who, device_id_type=MESH
        )

    top = pl.ds(wide - HALO, HALO)
    bottom = pl.ds(0, HALO)
    x_copies = [
        remote(polar_ref.at[:, top, :], low.at[0], xs.at[0], xr.at[0], x_right),
        remote(azimuth_ref.at[:, top, :], low.at[1], xs.at[1], xr.at[1], x_right),
        remote(classes_ref.at[:, :, top, :], lowk, xs.at[2], xr.at[2], x_right),
        remote(polar_ref.at[:, bottom, :], high.at[0], xs.at[3], xr.at[3], x_left),
        remote(azimuth_ref.at[:, bottom, :], high.at[1], xs.at[4], xr.at[4], x_left),
        remote(classes_ref.at[:, :, bottom, :], highk, xs.at[5], xr.at[5], x_left),
    ]
    for copy in x_copies:
        copy.start()

    lane = lax.broadcasted_iota(jnp.int32, (8, lanes), 1)
    group_of = lane // group
    place = lane % group

    def spread(z, polar, azimuth, classes_at, row):
        where_to = pl.ds(row, 8)
        shift = group * z + HALO
        mine = group_of == z
        spin = spins_of(polar, azimuth)
        for c in range(3):
            S[c, z + 1, where_to, :] = spin[c]
            old = pack[c, where_to, :]
            pack[c, where_to, :] = jnp.where(mine, pltpu.roll(spin[c], shift, 1), old)
        for d in range(6):
            value = lookup(classes_at(d), table_ref)
            J[d, z, where_to, :] = value
            old = pack[3 + d, where_to, :]
            pack[3 + d, where_to, :] = jnp.where(mine, pltpu.roll(value, shift, 1), old)

    pack[...] = jnp.zeros(pack.shape, jnp.float32)

    def own(z, carry):
        for r in range(inner):
            rows = pl.ds(8 * r, 8)
            spread(z, polar_ref[z, rows, :], azimuth_ref[z, rows, :],
                   lambda d: classes_ref[d, z, rows, :], HALO + 8 * r)
        return carry

    lax.fori_loop(0, depth, own, 0)

    def y_copies(part):
        rows = (pl.ds(HALO, wide), pl.ds(0, HALO), pl.ds(HALO + wide, HALO))[part]
        made = [remote(pack.at[:, rows, :], left_pack.at[:, rows, :], ys.at[part], yr.at[part], y_right)]
        if ny > 2:
            made.append(remote(pack.at[:, rows, :], right_pack.at[:, rows, :], ys.at[3 + part], yr.at[3 + part], y_left))
        return made

    def z_copies(field, base):
        return [
            remote(field.at[:, 1], field.at[:, depth + 1], zs.at[base], zr.at[base], z_down),
            remote(field.at[:, depth], field.at[:, 0], zs.at[base + 1], zr.at[base + 1], z_up),
        ]

    def g_copy(ghost, other, base):
        return remote(ghost, other, gs.at[base], gr.at[base], z_up)

    for copy in y_copies(0):
        copy.start()
    for copy in x_copies:
        copy.wait()

    def edges(z, carry):
        spread(z, low[0, z], low[1, z], lambda d: lowk[d, z], 0)
        spread(z, high[0, z], high[1, z], lambda d: highk[d, z], HALO + wide)
        return carry

    lax.fori_loop(0, depth, edges, 0)
    for part in (1, 2):
        for copy in y_copies(part):
            copy.start()
    for copy in z_copies(S, 0):
        copy.start()
    for part in range(3):
        for copy in y_copies(part):
            copy.wait()
    from_right = left_pack if ny == 2 else right_pack

    def ghosts(r, carry):
        rows = pl.ds(pl.multiple_of(8 * r, 8), 8)
        for f in range(9):
            value = jnp.where(place < HALO, left_pack[f, rows, :], from_right[f, rows, :])
            if f < 3:
                GS[f, rows, :] = value
            else:
                GJ[f - 3, rows, :] = value
        return carry

    lax.fori_loop(0, tiles, ghosts, 0)
    g_copy(GS, OS, 0).start()

    def x_pair(ref, r, value):
        if r < tiles - 1:
            ahead = ref[pl.ds(8 * r + 1, 8), :]
        else:
            ahead = pltpu.roll(value, 7, 0)
        if r > 0:
            behind = ref[pl.ds(8 * r - 1, 8), :]
        else:
            behind = pltpu.roll(value, 1, 0)
        return ahead, behind

    def plane(F, G, z, finish):
        up_shift = lanes - (group * z + HALO)
        left_mask = lane == group * z + HALO - 1
        right_mask = lane == group * z + HALO
        for r in range(tiles):
            rows = pl.ds(8 * r, 8)
            coupling = [J[d, z, rows, :] for d in range(6)]
            spin, field = [], []
            for c in range(3):
                M = F[c, z + 1, rows, :]
                ahead, behind = x_pair(F.at[c, z + 1], r, M)
                U = pltpu.roll(G[c, rows, :], up_shift, 1)
                right = pltpu.roll(jnp.where(lane == 0, U, M), lanes - 1, 1)
                left = pltpu.roll(jnp.where(lane == lanes - 1, U, M), 1, 1)
                total = coupling[0] * ahead + coupling[1] * right
                total = total + coupling[2] * F[c, z + 2, rows, :]
                total = total + coupling[3] * behind
                total = total + coupling[4] * left
                total = total + coupling[5] * F[c, z, rows, :]
                ins[c, rows, :] = jnp.where(
                    left_mask, pltpu.roll(M, group * z + HALO - 1, 1),
                    jnp.where(right_mask, pltpu.roll(M, group * z + HALO + 1, 1), ins[c, rows, :]))
                spin.append(M)
                field.append(total)
            finish(spin, velocity_of(spin, field), z, rows)

    def ghost_pass(G, other, finish):
        for r in range(tiles):
            rows = pl.ds(8 * r, 8)
            coupling = [GJ[d, rows, :] for d in range(6)]
            spin, field = [], []
            for c in range(3):
                M = G[c, rows, :]
                O = other[c, rows, :]
                I = ins[c, rows, :]
                ahead, behind = x_pair(G.at[c], r, M)
                right = jnp.where(place == HALO - 1, I, pltpu.roll(M, lanes - 1, 1))
                left = jnp.where(place == HALO, I, pltpu.roll(M, 1, 1))
                above = pltpu.roll(jnp.where(lane >= group, M, O), lanes - group, 1)
                below = pltpu.roll(jnp.where(lane < lanes - group, M, O), group, 1)
                total = coupling[0] * ahead + coupling[1] * right
                total = total + coupling[2] * above
                total = total + coupling[3] * behind
                total = total + coupling[4] * left
                total = total + coupling[5] * below
                spin.append(M)
                field.append(total)
            finish(spin, velocity_of(spin, field), rows)

    def predict(spin, speed, z, rows):
        for c in range(3):
            Q[c, z + 1, rows, :] = spin[c] + time_step * speed[c]

    def predict_ghost(spin, speed, rows):
        for c in range(3):
            GQ[c, rows, :] = spin[c] + time_step * speed[c]

    def correct(spin, speed, z, rows):
        for c in range(3):
            S[c, z + 1, rows, :] = 0.5 * (S[c, z + 1, rows, :] + spin[c]) + 0.5 * time_step * speed[c]

    def correct_ghost(spin, speed, rows):
        for c in range(3):
            GS[c, rows, :] = 0.5 * (GS[c, rows, :] + spin[c]) + 0.5 * time_step * speed[c]

    ins[...] = jnp.zeros(ins.shape, jnp.float32)

    def stage(F, G, O, base, finish, finish_ghost, send_main, send_ghost):
        def inside(z, carry):
            plane(F, G, z, finish)
            return carry

        def outside(i, carry):
            plane(F, G, i * (depth - 1), finish)
            return carry

        lax.fori_loop(1, depth - 1, inside, 0)
        for copy in z_copies(F, 2 * base):
            copy.wait()
        lax.fori_loop(0, 2, outside, 0)
        send_main()
        g_copy(G, O, base).wait()
        ghost_pass(G, O, finish_ghost)
        send_ghost()

    def out_copy(target):
        return pltpu.make_async_copy(S.at[:, pl.ds(1, depth), pl.ds(HALO, wide), :], target, osem.at[0])

    def step(turn, carry):
        def send_q():
            for copy in z_copies(Q, 2):
                copy.start()

        def send_s():
            @pl.when(turn < STEPS - 1)
            def _():
                for copy in z_copies(S, 0):
                    copy.start()

        def send_gs():
            @pl.when(turn < STEPS - 1)
            def _():
                g_copy(GS, OS, 0).start()

        stage(S, GS, OS, 0, predict, predict_ghost, send_q, lambda: g_copy(GQ, OQ, 1).start())

        @pl.when(turn == 2)
        def _():
            out_copy(mid_ref).wait()

        stage(Q, GQ, OQ, 1, correct, correct_ghost, send_s, send_gs)

        @pl.when(turn == 1)
        def _():
            out_copy(mid_ref).start()

        return carry

    lax.fori_loop(0, STEPS, step, 0)
    out_copy(end_ref).start()
    out_copy(end_ref).wait()


def evolve(polar_angle, azimuth, classes, exchange_table):
    depth, wide, lanes = polar_angle.shape
    sizes = (lax.axis_size("gx"), lax.axis_size("gy"), lax.axis_size("gz"))
    assert sizes[2] == 2 and depth * 2 * HALO == lanes
    ext = wide + 2 * HALO
    f32 = jnp.float32
    out = jax.ShapeDtypeStruct((3, depth, wide, lanes), f32)
    vmem = pl.BlockSpec(memory_space=pltpu.VMEM)
    anywhere = pl.BlockSpec(memory_space=pl.ANY)
    V = pltpu.VMEM
    D = pltpu.SemaphoreType.DMA
    return pl.pallas_call(
        functools.partial(evolve_kernel, sizes),
        out_shape=(out, out),
        in_specs=[vmem, vmem, vmem, pl.BlockSpec(memory_space=pltpu.SMEM)],
        out_specs=(anywhere, anywhere),
        scratch_shapes=[
            V((3, depth + 2, ext, lanes), f32), V((3, depth + 2, ext, lanes), f32),
            V((6, depth, ext, lanes), f32),
            V((3, ext, lanes), f32), V((3, ext, lanes), f32), V((6, ext, lanes), f32),
            V((3, ext, lanes), f32), V((3, ext, lanes), f32), V((3, ext, lanes), f32),
            V((2, depth, HALO, lanes), f32), V((2, depth, HALO, lanes), f32),
            V((6, depth, HALO, lanes), jnp.int32), V((6, depth, HALO, lanes), jnp.int32),
            V((9, ext, lanes), f32), V((9, ext, lanes), f32), V((9, ext, lanes), f32),
            D((6,)), D((6,)), D((6,)), D((6,)), D((4,)), D((4,)), D((2,)), D((2,)), D((1,)),
        ],
        compiler_params=pltpu.CompilerParams(collective_id=0, has_side_effects=True, vmem_limit_bytes=48 * 1024 * 1024),
        name="evolve",
    )(polar_angle, azimuth, classes, exchange_table)


def phase_table(wave_count, total_length):
    index = np.arange(total_length)[:, None] * np.arange(wave_count)[None, :] % total_length
    phase = index * (2.0 * math.pi / total_length)
    return np.cos(phase).astype(np.float32), np.sin(phase).astype(np.float32)


def exact_dot(a, b):
    return jnp.dot(a, b, precision=lax.Precision.HIGHEST, preferred_element_type=jnp.float32)


def modes_kernel(sizes, scale, mid_ref, end_ref, x_ref, y_ref, cos_ref, sin_ref, out_ref,
                 T, R, Z, D, DR, E, F, zs, zr, xs, xr, ys, yr, fs, fr):
    nx, ny, nz = sizes
    depth, wide, lanes = mid_ref.shape[1:]
    owned = D.shape[1]
    half = KX // nz
    me_x, me_y, me_z = lax.axis_index("gx"), lax.axis_index("gy"), lax.axis_index("gz")
    peers_x = [{"gx": lax.rem(me_x + o, nx)} for o in range(1, nx)]
    peers_y = [{"gy": lax.rem(me_y + o, ny)} for o in range(1, ny)]
    twin = {"gz": 1 - me_z}

    barrier = pltpu.get_barrier_semaphore()
    for who in peers_x + peers_y + [twin]:
        pl.semaphore_signal(barrier, inc=1, device_id=who, device_id_type=MESH)
    pl.semaphore_wait(barrier, nx + ny - 1)

    def remote(src, dst, send, recv, who):
        return pltpu.make_async_remote_copy(
            src_ref=src, dst_ref=dst, send_sem=send, recv_sem=recv, device_id=who, device_id_type=MESH
        )

    table = x_ref[...]
    for c in range(3):
        for z in range(depth):
            for turn, ref in enumerate((mid_ref, end_ref)):
                along_x = exact_dot(table, ref[c, z])
                T[pl.ds(z * KX, KX), pl.ds(2 * lanes * turn, lanes)] = along_x[:KX]
                T[pl.ds(z * KX, KX), pl.ds(2 * lanes * turn + lanes, lanes)] = along_x[KX:]
        parts = exact_dot(T[...], y_ref[...]).reshape(depth, nz, half, 4 * KY)
        for h in range(nz):
            R[h, c] = parts[:, h]
    swap = remote(R.at[1 - me_z], Z, zs.at[0], zr.at[0], twin)
    swap.start()
    swap.wait()

    lane = lax.broadcasted_iota(jnp.int32, (half, 4 * KY), 1)
    cosine_lane = (lane // KY) % 2 == 0

    def waves(block, carry):
        for c in range(3):
            ones, twos = [], []
            for z in range(nz * depth):
                own = R[me_z, c, z] if z < depth else Z[c, z - depth]
                ones.append(own)
                twos.append(jnp.where(cosine_lane, -pltpu.roll(own, 3 * KY, 1), pltpu.roll(own, KY, 1)))
            for k in range(owned):
                total = None
                for z in range(nz * depth):
                    where_z = me_z * depth + z if z < depth else (1 - me_z) * depth + z - depth
                    wave = block * owned + k
                    term = cos_ref[wave, where_z] * ones[z] + sin_ref[wave, where_z] * twos[z]
                    total = term if total is None else total + term
                D[block, k, c] = total
        return carry

    lax.fori_loop(0, nx, waves, 0)
    x_copies = [
        remote(D.at[lax.rem(me_x + o, nx)], DR.at[o - 1], xs.at[o - 1], xr.at[o - 1], peers_x[o - 1])
        for o in range(1, nx)
    ]
    for copy in x_copies:
        copy.start()
    for copy in x_copies:
        copy.wait()
    total = D[me_x]
    for o in range(1, nx):
        total = total + DR[o - 1]
    E[me_y] = total
    y_copies = [
        remote(E.at[me_y], E.at[me_y], ys.at[o - 1], yr.at[o - 1], peers_y[o - 1]) for o in range(1, ny)
    ]
    for copy in y_copies:
        copy.start()
    for copy in y_copies:
        copy.wait()
    total = E[0]
    for o in range(1, ny):
        total = total + E[o]
    F[me_z] = total * jnp.where(cosine_lane, scale, -scale)
    share = remote(F.at[me_z], F.at[me_z], fs.at[0], fr.at[0], twin)
    share.start()
    share.wait()
    out_ref[...] = F[...]


def modes(spin_mid, spin_end):
    depth, wide, lanes = spin_mid.shape[1:]
    sizes = nx, ny, nz = (lax.axis_size("gx"), lax.axis_size("gy"), lax.axis_size("gz"))
    total_z = depth * nz
    owned = total_z // nx
    half = KX // nz
    f32 = jnp.float32
    x_cos, x_sin = phase_table(KX, wide * nx)
    y_cos, y_sin = phase_table(KY, lanes * ny)
    z_cos, z_sin = phase_table(total_z, total_z)
    x_full = np.concatenate([x_cos, x_sin], 1).reshape(nx, wide, 2 * KX).transpose(0, 2, 1)
    y_pair = np.stack([
        np.concatenate([y_cos, y_sin], 1).reshape(ny, lanes, 2 * KY),
        np.concatenate([-y_sin, y_cos], 1).reshape(ny, lanes, 2 * KY),
    ], 1).reshape(ny, 2 * lanes, 2 * KY)
    y_full = np.zeros((ny, 4 * lanes, 4 * KY), np.float32)
    y_full[:, : 2 * lanes, : 2 * KY] = y_pair
    y_full[:, 2 * lanes :, 2 * KY :] = y_pair
    x_table = lax.dynamic_index_in_dim(jnp.asarray(x_full), lax.axis_index("gx"), 0, False)
    y_table = lax.dynamic_index_in_dim(jnp.asarray(y_full), lax.axis_index("gy"), 0, False)
    scale = float(wide * nx * lanes * ny * total_z) ** -0.5
    vmem = pl.BlockSpec(memory_space=pltpu.VMEM)
    smem = pl.BlockSpec(memory_space=pltpu.SMEM)
    V, DMA = pltpu.VMEM, pltpu.SemaphoreType.DMA
    width = 4 * KY
    out = pl.pallas_call(
        functools.partial(modes_kernel, sizes, scale),
        out_shape=jax.ShapeDtypeStruct((nz, owned, 3, half, width), f32),
        in_specs=[vmem, vmem, vmem, vmem, smem, smem],
        out_specs=vmem,
        scratch_shapes=[
            V((depth * KX, 4 * lanes), f32), V((nz, 3, depth, half, width), f32),
            V((3, depth, half, width), f32), V((nx, owned, 3, half, width), f32),
            V((nx - 1, owned, 3, half, width), f32), V((ny, owned, 3, half, width), f32),
            V((nz, owned, 3, half, width), f32),
            DMA((1,)), DMA((1,)), DMA((nx - 1,)), DMA((nx - 1,)), DMA((ny - 1,)), DMA((ny - 1,)),
            DMA((1,)), DMA((1,)),
        ],
        compiler_params=pltpu.CompilerParams(collective_id=1, has_side_effects=True, vmem_limit_bytes=32 * 1024 * 1024),
        name="modes",
    )(spin_mid, spin_end, x_table, y_table, jnp.asarray(z_cos.T), jnp.asarray(z_sin.T))
    out = out.reshape(nz, owned, 3, half, 2, 2, KY).transpose(4, 1, 5, 2, 0, 3, 6)
    return out.reshape(2, owned, -1)


def body(polar_angle, azimuth, classes, exchange_table):
    spin_mid, spin_end = evolve(polar_angle, azimuth, classes, exchange_table)
    both = modes(spin_mid, spin_end)
    return (spin_end, both[0], both[1])


def solution(mesh):
    return jax.shard_map(
        body,
        mesh=mesh,
        in_specs=(
            P("gz", ("groups", "gx"), "gy"),
            P("gz", ("groups", "gx"), "gy"),
            P(None, "gz", ("groups", "gx"), "gy"),
            P(),
        ),
        out_specs=(
            P(None, "gz", ("groups", "gx"), "gy"),
            P(("groups", "gx"), None),
            P(("groups", "gx"), None),
        ),
        check_vma=False,
    )
```

```python
import functools
import math

import jax
import jax.numpy as jnp
import numpy as np
from jax import lax
from jax.experimental import pallas as pl
from jax.experimental.pallas import tpu as pltpu
from jax.sharding import PartitionSpec as P

KX = 32
KY = 32
STEPS = 4
HALO = 8
MESH = pl.DeviceIdType.MESH

time_step = 0.1
damping = 0.1


def sin_cos(angle):
    turns = jnp.floor(angle * (2.0 / math.pi) + 0.5)
    rest = angle - turns * 1.5703125
    rest = rest - turns * 4.837512969970703125e-4
    rest = rest - turns * 7.54978995489188216e-8
    square = rest * rest
    sine = rest + rest * square * (
        -1.6666654611e-1 + square * (8.3321608736e-3 + square * -1.9515295891e-4)
    )
    cosine = (1.0 - 0.5 * square) + square * square * (
        4.166664568298827e-2 + square * (-1.388731625493765e-3 + square * 2.443315711809948e-5)
    )
    size = jnp.abs(turns)
    odd = size == 1.0
    half = size == 2.0
    sine_out = jnp.where(odd, jnp.where(turns > 0.0, cosine, -cosine), jnp.where(half, -sine, sine))
    cosine_out = jnp.where(odd, jnp.where(turns > 0.0, -sine, sine), jnp.where(half, -cosine, cosine))
    return sine_out, cosine_out


def spins_of(polar, azimuth):
    sine_polar, cosine_polar = sin_cos(polar)
    sine_azimuth, cosine_azimuth = sin_cos(azimuth)
    return sine_polar * cosine_azimuth, sine_polar * sine_azimuth, cosine_polar


def lookup(classes, table_ref):
    values = [table_ref[i] for i in range(table_ref.shape[0])]
    bit = 1
    level = None
    while len(values) > 1:
        mask = (classes & bit) != 0
        values = [
            jnp.where(mask, values[i + 1], values[i]) if i + 1 < len(values) else values[i]
            for i in range(0, len(values), 2)
        ]
        bit *= 2
    return values[0] + jnp.zeros(classes.shape, jnp.float32)


def velocity_of(spin, field):
    s0, s1, s2 = spin
    h0, h1, h2 = field
    t0 = s1 * h2 - s2 * h1
    t1 = s2 * h0 - s0 * h2
    t2 = s0 * h1 - s1 * h0
    return (
        -t0 - damping * (s1 * t2 - s2 * t1),
        -t1 - damping * (s2 * t0 - s0 * t2),
        -t2 - damping * (s0 * t1 - s1 * t0),
    )


def evolve_kernel(sizes, polar_in, azimuth_in, classes_in, table_ref, mid_ref, end_ref,
                  polar_ref, azimuth_ref, classes_ref, S, Q, J, GS, GQ, GJ, OS, OQ, ins, low, high, lowk, highk,
                  pack, left_pack, right_pack,
                  xs, xr, ys, yr, zs, zr, gs, gr, osem, isem):
    nx, ny, nz = sizes
    depth, wide, lanes = polar_ref.shape
    ext = wide + 2 * HALO
    tiles = ext // 8
    inner = wide // 8
    group = 2 * HALO
    me_x, me_y, me_z = lax.axis_index("gx"), lax.axis_index("gy"), lax.axis_index("gz")

    def at(axis, me, n, step):
        return {axis: lax.rem(me + (step + n), n)}

    x_left, x_right = at("gx", me_x, nx, -1), at("gx", me_x, nx, 1)
    y_left, y_right = at("gy", me_y, ny, -1), at("gy", me_y, ny, 1)
    z_down, z_up = at("gz", me_z, nz, -1), at("gz", me_z, nz, 1)

    fetches = [
        pltpu.make_async_copy(polar_in, polar_ref, isem.at[0]),
        pltpu.make_async_copy(azimuth_in, azimuth_ref, isem.at[1]),
        pltpu.make_async_copy(classes_in, classes_ref, isem.at[2]),
    ]
    for copy in fetches:
        copy.start()
    barrier = pltpu.get_barrier_semaphore()
    for who in (x_left, x_right, y_left, y_right, z_down, z_up):
        pl.semaphore_signal(barrier, inc=1, device_id=who, device_id_type=MESH)
    pl.semaphore_wait(barrier, 6)

    def remote(src, dst, send, recv, who):
        return pltpu.make_async_remote_copy(
            src_ref=src, dst_ref=dst, send_sem=send, recv_sem=recv, device_id=who, device_id_type=MESH
        )

    top = pl.ds(wide - HALO, HALO)
    bottom = pl.ds(0, HALO)
    x_copies = [
        remote(polar_in.at[:, top, :], low.at[0], xs.at[0], xr.at[0], x_right),
        remote(azimuth_in.at[:, top, :], low.at[1], xs.at[1], xr.at[1], x_right),
        remote(classes_in.at[:, :, top, :], lowk, xs.at[2], xr.at[2], x_right),
        remote(polar_in.at[:, bottom, :], high.at[0], xs.at[3], xr.at[3], x_left),
        remote(azimuth_in.at[:, bottom, :], high.at[1], xs.at[4], xr.at[4], x_left),
        remote(classes_in.at[:, :, bottom, :], highk, xs.at[5], xr.at[5], x_left),
    ]
    for copy in x_copies:
        copy.start()

    lane = lax.broadcasted_iota(jnp.int32, (8, lanes), 1)
    group_of = lane // group
    place = lane % group

    def spread(z, polar, azimuth, classes_at, row):
        where_to = pl.ds(row, 8)
        shift = group * z + HALO
        mine = group_of == z
        spin = spins_of(polar, azimuth)
        for c in range(3):
            S[c, z + 1, where_to, :] = spin[c]
            old = pack[c, where_to, :]
            pack[c, where_to, :] = jnp.where(mine, pltpu.roll(spin[c], shift, 1), old)
        for d in range(6):
            value = lookup(classes_at(d), table_ref)
            J[d, z, where_to, :] = value
            old = pack[3 + d, where_to, :]
            pack[3 + d, where_to, :] = jnp.where(mine, pltpu.roll(value, shift, 1), old)

    pack[...] = jnp.zeros(pack.shape, jnp.float32)

    def own(z, carry):
        for r in range(inner):
            rows = pl.ds(8 * r, 8)
            spread(z, polar_ref[z, rows, :], azimuth_ref[z, rows, :],
                   lambda d: classes_ref[d, z, rows, :], HALO + 8 * r)
        return carry

    for copy in fetches:
        copy.wait()
    lax.fori_loop(0, depth, own, 0)

    def y_copies(part):
        rows = (pl.ds(HALO, wide), pl.ds(0, HALO), pl.ds(HALO + wide, HALO))[part]
        made = [remote(pack.at[:, rows, :], left_pack.at[:, rows, :], ys.at[part], yr.at[part], y_right)]
        if ny > 2:
            made.append(remote(pack.at[:, rows, :], right_pack.at[:, rows, :], ys.at[3 + part], yr.at[3 + part], y_left))
        return made

    def z_copies(field, base):
        return [
            remote(field.at[:, 1], field.at[:, depth + 1], zs.at[base], zr.at[base], z_down),
            remote(field.at[:, depth], field.at[:, 0], zs.at[base + 1], zr.at[base + 1], z_up),
        ]

    def g_copy(ghost, other, base):
        return remote(ghost, other, gs.at[base], gr.at[base], z_up)

    for copy in y_copies(0):
        copy.start()
    for copy in x_copies:
        copy.wait()

    def edges(z, carry):
        spread(z, low[0, z], low[1, z], lambda d: lowk[d, z], 0)
        spread(z, high[0, z], high[1, z], lambda d: highk[d, z], HALO + wide)
        return carry

    lax.fori_loop(0, depth, edges, 0)
    for part in (1, 2):
        for copy in y_copies(part):
            copy.start()
    for copy in z_copies(S, 0):
        copy.start()
    for part in range(3):
        for copy in y_copies(part):
            copy.wait()
    from_right = left_pack if ny == 2 else right_pack

    def ghosts(r, carry):
        rows = pl.ds(pl.multiple_of(8 * r, 8), 8)
        for f in range(9):
            value = jnp.where(place < HALO, left_pack[f, rows, :], from_right[f, rows, :])
            if f < 3:
                GS[f, rows, :] = value
            else:
                GJ[f - 3, rows, :] = value
        return carry

    lax.fori_loop(0, tiles, ghosts, 0)
    g_copy(GS, OS, 0).start()

    def x_pair(ref, r, value):
        if r < tiles - 1:
            ahead = ref[pl.ds(8 * r + 1, 8), :]
        else:
            ahead = pltpu.roll(value, 7, 0)
        if r > 0:
            behind = ref[pl.ds(8 * r - 1, 8), :]
        else:
            behind = pltpu.roll(value, 1, 0)
        return ahead, behind

    def plane(F, G, z, finish):
        up_shift = lanes - (group * z + HALO)
        left_mask = lane == group * z + HALO - 1
        right_mask = lane == group * z + HALO
        for r in range(tiles):
            rows = pl.ds(8 * r, 8)
            coupling = [J[d, z, rows, :] for d in range(6)]
            spin, field = [], []
            for c in range(3):
                M = F[c, z + 1, rows, :]
                ahead, behind = x_pair(F.at[c, z + 1], r, M)
                U = pltpu.roll(G[c, rows, :], up_shift, 1)
                right = pltpu.roll(jnp.where(lane == 0, U, M), lanes - 1, 1)
                left = pltpu.roll(jnp.where(lane == lanes - 1, U, M), 1, 1)
                total = coupling[0] * ahead + coupling[1] * right
                total = total + coupling[2] * F[c, z + 2, rows, :]
                total = total + coupling[3] * behind
                total = total + coupling[4] * left
                total = total + coupling[5] * F[c, z, rows, :]
                ins[c, rows, :] = jnp.where(
                    left_mask, pltpu.roll(M, group * z + HALO - 1, 1),
                    jnp.where(right_mask, pltpu.roll(M, group * z + HALO + 1, 1), ins[c, rows, :]))
                spin.append(M)
                field.append(total)
            finish(spin, velocity_of(spin, field), z, rows)

    def ghost_pass(G, other, finish):
        for r in range(tiles):
            rows = pl.ds(8 * r, 8)
            coupling = [GJ[d, rows, :] for d in range(6)]
            spin, field = [], []
            for c in range(3):
                M = G[c, rows, :]
                O = other[c, rows, :]
                I = ins[c, rows, :]
                ahead, behind = x_pair(G.at[c], r, M)
                right = jnp.where(place == HALO - 1, I, pltpu.roll(M, lanes - 1, 1))
                left = jnp.where(place == HALO, I, pltpu.roll(M, 1, 1))
                above = pltpu.roll(jnp.where(lane >= group, M, O), lanes - group, 1)
                below = pltpu.roll(jnp.where(lane < lanes - group, M, O), group, 1)
                total = coupling[0] * ahead + coupling[1] * right
                total = total + coupling[2] * above
                total = total + coupling[3] * behind
                total = total + coupling[4] * left
                total = total + coupling[5] * below
                spin.append(M)
                field.append(total)
            finish(spin, velocity_of(spin, field), rows)

    def predict(spin, speed, z, rows):
        for c in range(3):
            Q[c, z + 1, rows, :] = spin[c] + time_step * speed[c]

    def predict_ghost(spin, speed, rows):
        for c in range(3):
            GQ[c, rows, :] = spin[c] + time_step * speed[c]

    def correct(spin, speed, z, rows):
        for c in range(3):
            S[c, z + 1, rows, :] = 0.5 * (S[c, z + 1, rows, :] + spin[c]) + 0.5 * time_step * speed[c]

    def correct_ghost(spin, speed, rows):
        for c in range(3):
            GS[c, rows, :] = 0.5 * (GS[c, rows, :] + spin[c]) + 0.5 * time_step * speed[c]

    ins[...] = jnp.zeros(ins.shape, jnp.float32)

    def stage(F, G, O, base, finish, finish_ghost, send_main, send_ghost):
        def inside(z, carry):
            plane(F, G, z, finish)
            return carry

        def outside(i, carry):
            plane(F, G, i * (depth - 1), finish)
            return carry

        lax.fori_loop(1, depth - 1, inside, 0)
        for copy in z_copies(F, 2 * base):
            copy.wait()
        lax.fori_loop(0, 2, outside, 0)
        send_main()
        g_copy(G, O, base).wait()
        ghost_pass(G, O, finish_ghost)
        send_ghost()

    def out_copy(target):
        return pltpu.make_async_copy(S.at[:, pl.ds(1, depth), pl.ds(HALO, wide), :], target, osem.at[0])

    def step(turn, carry):
        def send_q():
            for copy in z_copies(Q, 2):
                copy.start()

        def send_s():
            @pl.when(turn < STEPS - 1)
            def _():
                for copy in z_copies(S, 0):
                    copy.start()

        def send_gs():
            @pl.when(turn < STEPS - 1)
            def _():
                g_copy(GS, OS, 0).start()

        stage(S, GS, OS, 0, predict, predict_ghost, send_q, lambda: g_copy(GQ, OQ, 1).start())

        @pl.when(turn == 2)
        def _():
            out_copy(mid_ref).wait()

        stage(Q, GQ, OQ, 1, correct, correct_ghost, send_s, send_gs)

        @pl.when(turn == 1)
        def _():
            out_copy(mid_ref).start()

        return carry

    lax.fori_loop(0, STEPS, step, 0)
    out_copy(end_ref).start()
    out_copy(end_ref).wait()


def evolve(polar_angle, azimuth, classes, exchange_table):
    depth, wide, lanes = polar_angle.shape
    sizes = (lax.axis_size("gx"), lax.axis_size("gy"), lax.axis_size("gz"))
    assert sizes[2] == 2 and depth * 2 * HALO == lanes
    ext = wide + 2 * HALO
    f32 = jnp.float32
    out = jax.ShapeDtypeStruct((3, depth, wide, lanes), f32)
    hbm = pl.BlockSpec(memory_space=pltpu.HBM)
    anywhere = pl.BlockSpec(memory_space=pl.ANY)
    V = pltpu.VMEM
    D = pltpu.SemaphoreType.DMA
    return pl.pallas_call(
        functools.partial(evolve_kernel, sizes),
        out_shape=(out, out),
        in_specs=[hbm, hbm, hbm, pl.BlockSpec(memory_space=pltpu.SMEM)],
        out_specs=(anywhere, anywhere),
        scratch_shapes=[
            V((depth, wide, lanes), f32), V((depth, wide, lanes), f32), V((6, depth, wide, lanes), jnp.int32),
            V((3, depth + 2, ext, lanes), f32), V((3, depth + 2, ext, lanes), f32),
            V((6, depth, ext, lanes), f32),
            V((3, ext, lanes), f32), V((3, ext, lanes), f32), V((6, ext, lanes), f32),
            V((3, ext, lanes), f32), V((3, ext, lanes), f32), V((3, ext, lanes), f32),
            V((2, depth, HALO, lanes), f32), V((2, depth, HALO, lanes), f32),
            V((6, depth, HALO, lanes), jnp.int32), V((6, depth, HALO, lanes), jnp.int32),
            V((9, ext, lanes), f32), V((9, ext, lanes), f32), V((9, ext, lanes), f32),
            D((6,)), D((6,)), D((6,)), D((6,)), D((4,)), D((4,)), D((2,)), D((2,)), D((1,)), D((3,)),
        ],
        compiler_params=pltpu.CompilerParams(collective_id=0, has_side_effects=True, vmem_limit_bytes=48 * 1024 * 1024),
        name="evolve",
    )(polar_angle, azimuth, classes, exchange_table)


def phase_table(wave_count, total_length):
    index = np.arange(total_length)[:, None] * np.arange(wave_count)[None, :] % total_length
    phase = index * (2.0 * math.pi / total_length)
    return np.cos(phase).astype(np.float32), np.sin(phase).astype(np.float32)


def exact_dot(a, b):
    return jnp.dot(a, b, precision=lax.Precision.HIGHEST, preferred_element_type=jnp.float32)


def modes_kernel(sizes, scale, mid_ref, end_ref, x_in, y_in, cos_ref, sin_ref, out_ref,
                 x_ref, y_ref, T, R, Z, D, DR, E, F, zs, zr, xs, xr, ys, yr, fs, fr, isem):
    nx, ny, nz = sizes
    depth, wide, lanes = mid_ref.shape[1:]
    owned = D.shape[2]
    half = KX // nz
    me_x, me_y, me_z = lax.axis_index("gx"), lax.axis_index("gy"), lax.axis_index("gz")
    peers_x = [{"gx": lax.rem(me_x + o, nx)} for o in range(1, nx)]
    peers_y = [{"gy": lax.rem(me_y + o, ny)} for o in range(1, ny)]
    twin = {"gz": 1 - me_z}
    fetches = [
        pltpu.make_async_copy(x_in.at[me_x], x_ref, isem.at[0]),
        pltpu.make_async_copy(y_in.at[me_y], y_ref, isem.at[1]),
    ]
    for copy in fetches:
        copy.start()

    barrier = pltpu.get_barrier_semaphore()
    for who in peers_x + peers_y + [twin]:
        pl.semaphore_signal(barrier, inc=1, device_id=who, device_id_type=MESH)
    pl.semaphore_wait(barrier, nx + ny - 1)

    def remote(src, dst, send, recv, who):
        return pltpu.make_async_remote_copy(
            src_ref=src, dst_ref=dst, send_sem=send, recv_sem=recv, device_id=who, device_id_type=MESH
        )

    lane = lax.broadcasted_iota(jnp.int32, (half, 4 * KY), 1)
    cosine_lane = (lane // KY) % 2 == 0
    for copy in fetches:
        copy.wait()
    table = x_ref[...]
    swaps, x_copies, y_copies, shares = [], [], [], []

    def transform(c):
        for z in range(depth):
            for turn, ref in enumerate((mid_ref, end_ref)):
                along_x = exact_dot(table, ref[c, z])
                T[pl.ds(z * KX, KX), pl.ds(2 * lanes * turn, lanes)] = along_x[:KX]
                T[pl.ds(z * KX, KX), pl.ds(2 * lanes * turn + lanes, lanes)] = along_x[KX:]
        parts = exact_dot(T[...], y_ref[...]).reshape(depth, nz, half, 4 * KY)
        for h in range(nz):
            R[h, c] = parts[:, h]
        swaps.append(remote(R.at[1 - me_z, c], Z.at[c], zs.at[c], zr.at[c], twin))
        swaps[c].start()

    def waves(c):
        swaps[c].wait()
        ones, twos = [], []
        for z in range(nz * depth):
            own = R[me_z, c, z] if z < depth else Z[c, z - depth]
            ones.append(own)
            twos.append(jnp.where(cosine_lane, -pltpu.roll(own, 3 * KY, 1), pltpu.roll(own, KY, 1)))

        def block_of(block, carry):
            for k in range(owned):
                total = None
                for z in range(nz * depth):
                    where_z = me_z * depth + z if z < depth else (1 - me_z) * depth + z - depth
                    wave = block * owned + k
                    term = cos_ref[wave, where_z] * ones[z] + sin_ref[wave, where_z] * twos[z]
                    total = term if total is None else total + term
                D[c, block, k] = total
            return carry

        lax.fori_loop(0, nx, block_of, 0)
        x_copies.append([
            remote(D.at[c, lax.rem(me_x + o, nx)], DR.at[c, o - 1], xs.at[c, o - 1], xr.at[c, o - 1], peers_x[o - 1])
            for o in range(1, nx)
        ])
        for copy in reversed(x_copies[c]):
            copy.start()

    def sum_x(c):
        for copy in x_copies[c]:
            copy.wait()
        total = D[c, me_x]
        for o in range(1, nx):
            total = total + DR[c, o - 1]
        E[c, me_y] = total
        y_copies.append([
            remote(E.at[c, me_y], E.at[c, me_y], ys.at[c, o - 1], yr.at[c, o - 1], peers_y[o - 1])
            for o in range(1, ny)
        ])
        for copy in y_copies[c]:
            copy.start()

    def sum_y(c):
        for copy in y_copies[c]:
            copy.wait()
        total = E[c, 0]
        for o in range(1, ny):
            total = total + E[c, o]
        F[c, me_z] = total * jnp.where(cosine_lane, scale, -scale)
        shares.append(remote(F.at[c, me_z], F.at[c, me_z], fs.at[c], fr.at[c], twin))
        shares[c].start()

    transform(0)
    transform(1)
    waves(0)
    transform(2)
    waves(1)
    waves(2)
    sum_x(0)
    sum_x(1)
    sum_y(0)
    sum_x(2)
    sum_y(1)
    sum_y(2)
    for c in range(3):
        shares[c].wait()
        out_ref[:, :, c] = F[c]


def modes(spin_mid, spin_end):
    depth, wide, lanes = spin_mid.shape[1:]
    sizes = nx, ny, nz = (lax.axis_size("gx"), lax.axis_size("gy"), lax.axis_size("gz"))
    total_z = depth * nz
    owned = total_z // nx
    half = KX // nz
    f32 = jnp.float32
    x_cos, x_sin = phase_table(KX, wide * nx)
    y_cos, y_sin = phase_table(KY, lanes * ny)
    z_cos, z_sin = phase_table(total_z, total_z)
    x_full = np.concatenate([x_cos, x_sin], 1).reshape(nx, wide, 2 * KX).transpose(0, 2, 1)
    y_pair = np.stack([
        np.concatenate([y_cos, y_sin], 1).reshape(ny, lanes, 2 * KY),
        np.concatenate([-y_sin, y_cos], 1).reshape(ny, lanes, 2 * KY),
    ], 1).reshape(ny, 2 * lanes, 2 * KY)
    y_full = np.zeros((ny, 4 * lanes, 4 * KY), np.float32)
    y_full[:, : 2 * lanes, : 2 * KY] = y_pair
    y_full[:, 2 * lanes :, 2 * KY :] = y_pair
    scale = float(wide * nx * lanes * ny * total_z) ** -0.5
    vmem = pl.BlockSpec(memory_space=pltpu.VMEM)
    smem = pl.BlockSpec(memory_space=pltpu.SMEM)
    hbm = pl.BlockSpec(memory_space=pltpu.HBM)
    V, DMA = pltpu.VMEM, pltpu.SemaphoreType.DMA
    width = 4 * KY
    out = pl.pallas_call(
        functools.partial(modes_kernel, sizes, scale),
        out_shape=jax.ShapeDtypeStruct((nz, owned, 3, half, width), f32),
        in_specs=[vmem, vmem, hbm, hbm, smem, smem],
        out_specs=vmem,
        scratch_shapes=[
            V((2 * KX, wide), f32), V((4 * lanes, width), f32),
            V((depth * KX, 4 * lanes), f32), V((nz, 3, depth, half, width), f32),
            V((3, depth, half, width), f32), V((3, nx, owned, half, width), f32),
            V((3, nx - 1, owned, half, width), f32), V((3, ny, owned, half, width), f32),
            V((3, nz, owned, half, width), f32),
            DMA((3,)), DMA((3,)), DMA((3, nx - 1)), DMA((3, nx - 1)), DMA((3, ny - 1)), DMA((3, ny - 1)),
            DMA((3,)), DMA((3,)), DMA((2,)),
        ],
        compiler_params=pltpu.CompilerParams(collective_id=1, has_side_effects=True, vmem_limit_bytes=32 * 1024 * 1024),
        name="modes",
    )(spin_mid, spin_end, jnp.asarray(x_full), jnp.asarray(y_full), jnp.asarray(z_cos.T), jnp.asarray(z_sin.T))
    out = out.reshape(nz, owned, 3, half, 2, 2, KY).transpose(4, 1, 5, 2, 0, 3, 6)
    return out.reshape(2, owned, -1)


def body(polar_angle, azimuth, classes, exchange_table):
    spin_mid, spin_end = evolve(polar_angle, azimuth, classes, exchange_table)
    both = modes(spin_mid, spin_end)
    return (spin_end, both[0], both[1])


def solution(mesh):
    return jax.shard_map(
        body,
        mesh=mesh,
        in_specs=(
            P("gz", ("groups", "gx"), "gy"),
            P("gz", ("groups", "gx"), "gy"),
            P(None, "gz", ("groups", "gx"), "gy"),
            P(),
        ),
        out_specs=(
            P(None, "gz", ("groups", "gx"), "gy"),
            P(("groups", "gx"), None),
            P(("groups", "gx"), None),
        ),
        check_vma=False,
    )
```

```python
import functools
import math

import jax
import jax.numpy as jnp
import numpy as np
from jax import lax
from jax.experimental import pallas as pl
from jax.experimental.pallas import tpu as pltpu
from jax.sharding import PartitionSpec as P

KX = 32
KY = 32
STEPS = 4
HALO = 8
MESH = pl.DeviceIdType.MESH

time_step = 0.1
damping = 0.1


def sin_cos(angle):
    turns = jnp.floor(angle * (2.0 / math.pi) + 0.5)
    rest = angle - turns * 1.5703125
    rest = rest - turns * 4.837512969970703125e-4
    rest = rest - turns * 7.54978995489188216e-8
    square = rest * rest
    sine = rest + rest * square * (
        -1.6666654611e-1 + square * (8.3321608736e-3 + square * -1.9515295891e-4)
    )
    cosine = (1.0 - 0.5 * square) + square * square * (
        4.166664568298827e-2 + square * (-1.388731625493765e-3 + square * 2.443315711809948e-5)
    )
    size = jnp.abs(turns)
    odd = size == 1.0
    half = size == 2.0
    sine_out = jnp.where(odd, jnp.where(turns > 0.0, cosine, -cosine), jnp.where(half, -sine, sine))
    cosine_out = jnp.where(odd, jnp.where(turns > 0.0, -sine, sine), jnp.where(half, -cosine, cosine))
    return sine_out, cosine_out


def spins_of(polar, azimuth):
    sine_polar, cosine_polar = sin_cos(polar)
    sine_azimuth, cosine_azimuth = sin_cos(azimuth)
    return sine_polar * cosine_azimuth, sine_polar * sine_azimuth, cosine_polar


def lookup(classes, table_ref):
    values = [table_ref[i] for i in range(table_ref.shape[0])]
    bit = 1
    level = None
    while len(values) > 1:
        mask = (classes & bit) != 0
        values = [
            jnp.where(mask, values[i + 1], values[i]) if i + 1 < len(values) else values[i]
            for i in range(0, len(values), 2)
        ]
        bit *= 2
    return values[0] + jnp.zeros(classes.shape, jnp.float32)


def velocity_of(spin, field):
    s0, s1, s2 = spin
    h0, h1, h2 = field
    t0 = s1 * h2 - s2 * h1
    t1 = s2 * h0 - s0 * h2
    t2 = s0 * h1 - s1 * h0
    return (
        -t0 - damping * (s1 * t2 - s2 * t1),
        -t1 - damping * (s2 * t0 - s0 * t2),
        -t2 - damping * (s0 * t1 - s1 * t0),
    )


def evolve_kernel(sizes, polar_in, azimuth_in, classes_in, table_ref, mid_ref, end_ref,
                  polar_ref, azimuth_ref, classes_ref, S, Q, J, GS, GQ, GJ, OS, OQ, ins, low, high, lowk, highk,
                  pack, left_pack, right_pack,
                  xs, xr, ys, yr, zs, zr, gs, gr, osem, isem):
    nx, ny, nz = sizes
    depth, wide, lanes = polar_ref.shape
    ext = wide + 2 * HALO
    tiles = ext // 8
    inner = wide // 8
    group = 2 * HALO
    me_x, me_y, me_z = lax.axis_index("gx"), lax.axis_index("gy"), lax.axis_index("gz")

    def at(axis, me, n, step):
        return {axis: lax.rem(me + (step + n), n)}

    x_left, x_right = at("gx", me_x, nx, -1), at("gx", me_x, nx, 1)
    y_left, y_right = at("gy", me_y, ny, -1), at("gy", me_y, ny, 1)
    z_down, z_up = at("gz", me_z, nz, -1), at("gz", me_z, nz, 1)

    fetches = [
        pltpu.make_async_copy(polar_in, polar_ref, isem.at[0]),
        pltpu.make_async_copy(azimuth_in, azimuth_ref, isem.at[1]),
        pltpu.make_async_copy(classes_in, classes_ref, isem.at[2]),
    ]
    for copy in fetches:
        copy.start()
    barrier = pltpu.get_barrier_semaphore()
    for who in (x_left, x_right, y_left, y_right, z_down, z_up):
        pl.semaphore_signal(barrier, inc=1, device_id=who, device_id_type=MESH)
    pl.semaphore_wait(barrier, 6)

    def remote(src, dst, send, recv, who):
        return pltpu.make_async_remote_copy(
            src_ref=src, dst_ref=dst, send_sem=send, recv_sem=recv, device_id=who, device_id_type=MESH
        )

    top = pl.ds(wide - HALO, HALO)
    bottom = pl.ds(0, HALO)
    x_copies = [
        remote(polar_in.at[:, top, :], low.at[0], xs.at[0], xr.at[0], x_right),
        remote(azimuth_in.at[:, top, :], low.at[1], xs.at[1], xr.at[1], x_right),
        remote(classes_in.at[pl.ds(0, 3), :, top, :], lowk.at[pl.ds(0, 3)], xs.at[2], xr.at[2], x_right),
        remote(classes_in.at[4, :, top, :], lowk.at[4], xs.at[6], xr.at[6], x_right),
        remote(classes_in.at[5, 0, top, :], lowk.at[5, 0], xs.at[7], xr.at[7], x_right),
        remote(polar_in.at[:, bottom, :], high.at[0], xs.at[3], xr.at[3], x_left),
        remote(azimuth_in.at[:, bottom, :], high.at[1], xs.at[4], xr.at[4], x_left),
        remote(classes_in.at[pl.ds(0, 3), :, bottom, :], highk.at[pl.ds(0, 3)], xs.at[5], xr.at[5], x_left),
        remote(classes_in.at[4, :, bottom, :], highk.at[4], xs.at[8], xr.at[8], x_left),
        remote(classes_in.at[5, 0, bottom, :], highk.at[5, 0], xs.at[9], xr.at[9], x_left),
    ]
    for copy in x_copies:
        copy.start()

    lane = lax.broadcasted_iota(jnp.int32, (8, lanes), 1)
    group_of = lane // group
    place = lane % group

    def spread(z, polar, azimuth, coupling_at, row):
        where_to = pl.ds(row, 8)
        shift = group * z + HALO
        mine = group_of == z
        spin = spins_of(polar, azimuth)
        for c in range(3):
            S[c, z + 1, where_to, :] = spin[c]
            old = pack[c, where_to, :]
            pack[c, where_to, :] = jnp.where(mine, pltpu.roll(spin[c], shift, 1), old)
        for d in range(6):
            value = coupling_at(d)
            J[d, z, where_to, :] = value
            old = pack[3 + d, where_to, :]
            pack[3 + d, where_to, :] = jnp.where(mine, pltpu.roll(value, shift, 1), old)

    pack[...] = jnp.zeros(pack.shape, jnp.float32)

    def own(z, carry):
        for r in range(inner):
            rows = pl.ds(8 * r, 8)
            spread(z, polar_ref[z, rows, :], azimuth_ref[z, rows, :],
                   lambda d: lookup(classes_ref[d, z, rows, :], table_ref), HALO + 8 * r)
        return carry

    for copy in fetches:
        copy.wait()
    lax.fori_loop(0, depth, own, 0)

    def y_copies(part):
        rows = (pl.ds(HALO, wide), pl.ds(0, HALO), pl.ds(HALO + wide, HALO))[part]
        made = [remote(pack.at[:, rows, :], left_pack.at[:, rows, :], ys.at[part], yr.at[part], y_right)]
        if ny > 2:
            made.append(remote(pack.at[:, rows, :], right_pack.at[:, rows, :], ys.at[3 + part], yr.at[3 + part], y_left))
        return made

    def z_copies(field, base):
        return [
            remote(field.at[:, 1], field.at[:, depth + 1], zs.at[base], zr.at[base], z_down),
            remote(field.at[:, depth], field.at[:, 0], zs.at[base + 1], zr.at[base + 1], z_up),
        ]

    def g_copy(ghost, other, base):
        return remote(ghost, other, gs.at[base], gr.at[base], z_up)

    for copy in y_copies(0):
        copy.start()
    for copy in x_copies:
        copy.wait()

    def edges(z, carry):
        def coupling_at(halo, row, d):
            if d == 3 and row > 0:
                return J[0, z, pl.ds(row - 1, 8), :]
            if d == 3:
                return pltpu.roll(J[0, z, pl.ds(row, 8), :], 1, 0)
            if d == 5:
                below = J[2, jnp.maximum(z - 1, 0), pl.ds(row, 8), :]
                return jnp.where(z == 0, lookup(halo[5, 0], table_ref), below)
            return lookup(halo[d, z], table_ref)

        spread(z, low[0, z], low[1, z], lambda d: coupling_at(lowk, 0, d), 0)
        spread(z, high[0, z], high[1, z], lambda d: coupling_at(highk, HALO + wide, d), HALO + wide)
        return carry

    lax.fori_loop(0, depth, edges, 0)
    for part in (1, 2):
        for copy in y_copies(part):
            copy.start()
    for copy in z_copies(S, 0):
        copy.start()
    for part in range(3):
        for copy in y_copies(part):
            copy.wait()
    from_right = left_pack if ny == 2 else right_pack

    def ghosts(r, carry):
        rows = pl.ds(pl.multiple_of(8 * r, 8), 8)
        for f in range(9):
            value = jnp.where(place < HALO, left_pack[f, rows, :], from_right[f, rows, :])
            if f < 3:
                GS[f, rows, :] = value
            else:
                GJ[f - 3, rows, :] = value
        return carry

    lax.fori_loop(0, tiles, ghosts, 0)
    g_copy(GS, OS, 0).start()

    def x_pair(ref, r, value):
        if r < tiles - 1:
            ahead = ref[pl.ds(8 * r + 1, 8), :]
        else:
            ahead = pltpu.roll(value, 7, 0)
        if r > 0:
            behind = ref[pl.ds(8 * r - 1, 8), :]
        else:
            behind = pltpu.roll(value, 1, 0)
        return ahead, behind

    def plane(F, G, z, finish):
        up_shift = lanes - (group * z + HALO)
        left_mask = lane == group * z + HALO - 1
        right_mask = lane == group * z + HALO
        for r in range(tiles):
            rows = pl.ds(8 * r, 8)
            coupling = [J[d, z, rows, :] for d in range(6)]
            spin, field = [], []
            for c in range(3):
                M = F[c, z + 1, rows, :]
                ahead, behind = x_pair(F.at[c, z + 1], r, M)
                U = pltpu.roll(G[c, rows, :], up_shift, 1)
                right = pltpu.roll(jnp.where(lane == 0, U, M), lanes - 1, 1)
                left = pltpu.roll(jnp.where(lane == lanes - 1, U, M), 1, 1)
                total = coupling[0] * ahead + coupling[1] * right
                total = total + coupling[2] * F[c, z + 2, rows, :]
                total = total + coupling[3] * behind
                total = total + coupling[4] * left
                total = total + coupling[5] * F[c, z, rows, :]
                ins[c, rows, :] = jnp.where(
                    left_mask, pltpu.roll(M, group * z + HALO - 1, 1),
                    jnp.where(right_mask, pltpu.roll(M, group * z + HALO + 1, 1), ins[c, rows, :]))
                spin.append(M)
                field.append(total)
            finish(spin, velocity_of(spin, field), z, rows)

    def ghost_pass(G, other, finish):
        for r in range(tiles):
            rows = pl.ds(8 * r, 8)
            coupling = [GJ[d, rows, :] for d in range(6)]
            spin, field = [], []
            for c in range(3):
                M = G[c, rows, :]
                O = other[c, rows, :]
                I = ins[c, rows, :]
                ahead, behind = x_pair(G.at[c], r, M)
                right = jnp.where(place == HALO - 1, I, pltpu.roll(M, lanes - 1, 1))
                left = jnp.where(place == HALO, I, pltpu.roll(M, 1, 1))
                above = pltpu.roll(jnp.where(lane >= group, M, O), lanes - group, 1)
                below = pltpu.roll(jnp.where(lane < lanes - group, M, O), group, 1)
                total = coupling[0] * ahead + coupling[1] * right
                total = total + coupling[2] * above
                total = total + coupling[3] * behind
                total = total + coupling[4] * left
                total = total + coupling[5] * below
                spin.append(M)
                field.append(total)
            finish(spin, velocity_of(spin, field), rows)

    def predict(spin, speed, z, rows):
        for c in range(3):
            Q[c, z + 1, rows, :] = spin[c] + time_step * speed[c]

    def predict_ghost(spin, speed, rows):
        for c in range(3):
            GQ[c, rows, :] = spin[c] + time_step * speed[c]

    def correct(spin, speed, z, rows):
        for c in range(3):
            S[c, z + 1, rows, :] = 0.5 * (S[c, z + 1, rows, :] + spin[c]) + 0.5 * time_step * speed[c]

    def correct_ghost(spin, speed, rows):
        for c in range(3):
            GS[c, rows, :] = 0.5 * (GS[c, rows, :] + spin[c]) + 0.5 * time_step * speed[c]

    ins[...] = jnp.zeros(ins.shape, jnp.float32)

    def stage(F, G, O, base, finish, finish_ghost, send_main, send_ghost):
        def inside(z, carry):
            plane(F, G, z, finish)
            return carry

        def outside(i, carry):
            plane(F, G, i * (depth - 1), finish)
            return carry

        lax.fori_loop(1, depth - 1, inside, 0)
        for copy in z_copies(F, 2 * base):
            copy.wait()
        lax.fori_loop(0, 2, outside, 0)
        send_main()
        g_copy(G, O, base).wait()
        ghost_pass(G, O, finish_ghost)
        send_ghost()

    def out_copy(target):
        return pltpu.make_async_copy(S.at[:, pl.ds(1, depth), pl.ds(HALO, wide), :], target, osem.at[0])

    def step(turn, carry):
        def send_q():
            for copy in z_copies(Q, 2):
                copy.start()

        def send_s():
            @pl.when(turn < STEPS - 1)
            def _():
                for copy in z_copies(S, 0):
                    copy.start()

        def send_gs():
            @pl.when(turn < STEPS - 1)
            def _():
                g_copy(GS, OS, 0).start()

        stage(S, GS, OS, 0, predict, predict_ghost, send_q, lambda: g_copy(GQ, OQ, 1).start())

        @pl.when(turn == 2)
        def _():
            out_copy(mid_ref).wait()

        stage(Q, GQ, OQ, 1, correct, correct_ghost, send_s, send_gs)

        @pl.when(turn == 1)
        def _():
            out_copy(mid_ref).start()

        return carry

    lax.fori_loop(0, STEPS, step, 0)
    out_copy(end_ref).start()
    out_copy(end_ref).wait()


def evolve(polar_angle, azimuth, classes, exchange_table):
    depth, wide, lanes = polar_angle.shape
    sizes = (lax.axis_size("gx"), lax.axis_size("gy"), lax.axis_size("gz"))
    assert sizes[2] == 2 and depth * 2 * HALO == lanes
    ext = wide + 2 * HALO
    f32 = jnp.float32
    out = jax.ShapeDtypeStruct((3, depth, wide, lanes), f32)
    hbm = pl.BlockSpec(memory_space=pltpu.HBM)
    anywhere = pl.BlockSpec(memory_space=pl.ANY)
    V = pltpu.VMEM
    D = pltpu.SemaphoreType.DMA
    return pl.pallas_call(
        functools.partial(evolve_kernel, sizes),
        out_shape=(out, out),
        in_specs=[hbm, hbm, hbm, pl.BlockSpec(memory_space=pltpu.SMEM)],
        out_specs=(anywhere, anywhere),
        scratch_shapes=[
            V((depth, wide, lanes), f32), V((depth, wide, lanes), f32), V((6, depth, wide, lanes), jnp.int32),
            V((3, depth + 2, ext, lanes), f32), V((3, depth + 2, ext, lanes), f32),
            V((6, depth, ext, lanes), f32),
            V((3, ext, lanes), f32), V((3, ext, lanes), f32), V((6, ext, lanes), f32),
            V((3, ext, lanes), f32), V((3, ext, lanes), f32), V((3, ext, lanes), f32),
            V((2, depth, HALO, lanes), f32), V((2, depth, HALO, lanes), f32),
            V((6, depth, HALO, lanes), jnp.int32), V((6, depth, HALO, lanes), jnp.int32),
            V((9, ext, lanes), f32), V((9, ext, lanes), f32), V((9, ext, lanes), f32),
            D((10,)), D((10,)), D((6,)), D((6,)), D((4,)), D((4,)), D((2,)), D((2,)), D((1,)), D((3,)),
        ],
        compiler_params=pltpu.CompilerParams(collective_id=0, has_side_effects=True, vmem_limit_bytes=65200000),
        name="evolve",
    )(polar_angle, azimuth, classes, exchange_table)


def phase_table(wave_count, total_length):
    index = np.arange(total_length)[:, None] * np.arange(wave_count)[None, :] % total_length
    phase = index * (2.0 * math.pi / total_length)
    return np.cos(phase).astype(np.float32), np.sin(phase).astype(np.float32)


def exact_dot(a, b):
    return jnp.dot(a, b, precision=lax.Precision.HIGHEST, preferred_element_type=jnp.float32)


def modes_kernel(sizes, scale, mid_ref, end_ref, x_in, y_in, cos_ref, sin_ref, out_ref,
                 x_ref, y_ref, T, R, Z, D, DR, E, F, zs, zr, xs, xr, ys, yr, fs, fr, isem):
    nx, ny, nz = sizes
    depth, wide, lanes = mid_ref.shape[1:]
    owned = D.shape[2]
    half = KX // nz
    me_x, me_y, me_z = lax.axis_index("gx"), lax.axis_index("gy"), lax.axis_index("gz")
    peers_x = [{"gx": lax.rem(me_x + o, nx)} for o in range(1, nx)]
    peers_y = [{"gy": lax.rem(me_y + o, ny)} for o in range(1, ny)]
    twin = {"gz": 1 - me_z}
    fetches = [
        pltpu.make_async_copy(x_in.at[me_x], x_ref, isem.at[0]),
        pltpu.make_async_copy(y_in.at[me_y], y_ref, isem.at[1]),
    ]
    for copy in fetches:
        copy.start()

    barrier = pltpu.get_barrier_semaphore()
    for who in peers_x + peers_y + [twin]:
        pl.semaphore_signal(barrier, inc=1, device_id=who, device_id_type=MESH)
    pl.semaphore_wait(barrier, nx + ny - 1)

    def remote(src, dst, send, recv, who):
        return pltpu.make_async_remote_copy(
            src_ref=src, dst_ref=dst, send_sem=send, recv_sem=recv, device_id=who, device_id_type=MESH
        )

    lane = lax.broadcasted_iota(jnp.int32, (half, 4 * KY), 1)
    cosine_lane = (lane // KY) % 2 == 0
    for copy in fetches:
        copy.wait()
    table = x_ref[...]
    swaps, x_copies, y_copies, shares = [], [], [], []

    def transform(c):
        for z in range(depth):
            for turn, ref in enumerate((mid_ref, end_ref)):
                along_x = exact_dot(table, ref[c, z])
                T[pl.ds(z * KX, KX), pl.ds(2 * lanes * turn, lanes)] = along_x[:KX]
                T[pl.ds(z * KX, KX), pl.ds(2 * lanes * turn + lanes, lanes)] = along_x[KX:]
        parts = exact_dot(T[...], y_ref[...]).reshape(depth, nz, half, 4 * KY)
        for h in range(nz):
            R[h, c] = parts[:, h]
        swaps.append(remote(R.at[1 - me_z, c], Z.at[c], zs.at[c], zr.at[c], twin))
        swaps[c].start()

    def waves(c):
        swaps[c].wait()
        ones, twos = [], []
        for z in range(nz * depth):
            own = R[me_z, c, z] if z < depth else Z[c, z - depth]
            ones.append(own)
            twos.append(jnp.where(cosine_lane, -pltpu.roll(own, 3 * KY, 1), pltpu.roll(own, KY, 1)))

        def block_of(block, carry):
            for k in range(owned):
                total = None
                for z in range(nz * depth):
                    where_z = me_z * depth + z if z < depth else (1 - me_z) * depth + z - depth
                    wave = block * owned + k
                    term = cos_ref[wave, where_z] * ones[z] + sin_ref[wave, where_z] * twos[z]
                    total = term if total is None else total + term
                D[c, block, k] = total
            return carry

        lax.fori_loop(0, nx, block_of, 0)
        x_copies.append([
            remote(D.at[c, lax.rem(me_x + o, nx)], DR.at[c, o - 1], xs.at[c, o - 1], xr.at[c, o - 1], peers_x[o - 1])
            for o in range(1, nx)
        ])
        for copy in reversed(x_copies[c]):
            copy.start()

    def sum_x(c):
        for copy in x_copies[c]:
            copy.wait()
        total = D[c, me_x]
        for o in range(1, nx):
            total = total + DR[c, o - 1]
        E[c, me_y] = total
        y_copies.append([
            remote(E.at[c, me_y], E.at[c, me_y], ys.at[c, o - 1], yr.at[c, o - 1], peers_y[o - 1])
            for o in range(1, ny)
        ])
        for copy in y_copies[c]:
            copy.start()

    def sum_y(c):
        for copy in y_copies[c]:
            copy.wait()
        total = E[c, 0]
        for o in range(1, ny):
            total = total + E[c, o]
        F[c, me_z] = total * jnp.where(cosine_lane, scale, -scale)
        shares.append(remote(F.at[c, me_z], F.at[c, me_z], fs.at[c], fr.at[c], twin))
        shares[c].start()

    transform(0)
    transform(1)
    waves(0)
    transform(2)
    waves(1)
    waves(2)
    sum_x(0)
    sum_x(1)
    sum_y(0)
    sum_x(2)
    sum_y(1)
    sum_y(2)
    for c in range(3):
        shares[c].wait()
        out_ref[:, :, c] = F[c]


def modes(spin_mid, spin_end):
    depth, wide, lanes = spin_mid.shape[1:]
    sizes = nx, ny, nz = (lax.axis_size("gx"), lax.axis_size("gy"), lax.axis_size("gz"))
    total_z = depth * nz
    owned = total_z // nx
    half = KX // nz
    f32 = jnp.float32
    x_cos, x_sin = phase_table(KX, wide * nx)
    y_cos, y_sin = phase_table(KY, lanes * ny)
    z_cos, z_sin = phase_table(total_z, total_z)
    x_full = np.concatenate([x_cos, x_sin], 1).reshape(nx, wide, 2 * KX).transpose(0, 2, 1)
    y_pair = np.stack([
        np.concatenate([y_cos, y_sin], 1).reshape(ny, lanes, 2 * KY),
        np.concatenate([-y_sin, y_cos], 1).reshape(ny, lanes, 2 * KY),
    ], 1).reshape(ny, 2 * lanes, 2 * KY)
    y_full = np.zeros((ny, 4 * lanes, 4 * KY), np.float32)
    y_full[:, : 2 * lanes, : 2 * KY] = y_pair
    y_full[:, 2 * lanes :, 2 * KY :] = y_pair
    scale = float(wide * nx * lanes * ny * total_z) ** -0.5
    vmem = pl.BlockSpec(memory_space=pltpu.VMEM)
    smem = pl.BlockSpec(memory_space=pltpu.SMEM)
    hbm = pl.BlockSpec(memory_space=pltpu.HBM)
    V, DMA = pltpu.VMEM, pltpu.SemaphoreType.DMA
    width = 4 * KY
    out = pl.pallas_call(
        functools.partial(modes_kernel, sizes, scale),
        out_shape=jax.ShapeDtypeStruct((nz, owned, 3, half, width), f32),
        in_specs=[vmem, vmem, hbm, hbm, smem, smem],
        out_specs=vmem,
        scratch_shapes=[
            V((2 * KX, wide), f32), V((4 * lanes, width), f32),
            V((depth * KX, 4 * lanes), f32), V((nz, 3, depth, half, width), f32),
            V((3, depth, half, width), f32), V((3, nx, owned, half, width), f32),
            V((3, nx - 1, owned, half, width), f32), V((3, ny, owned, half, width), f32),
            V((3, nz, owned, half, width), f32),
            DMA((3,)), DMA((3,)), DMA((3, nx - 1)), DMA((3, nx - 1)), DMA((3, ny - 1)), DMA((3, ny - 1)),
            DMA((3,)), DMA((3,)), DMA((2,)),
        ],
        compiler_params=pltpu.CompilerParams(collective_id=1, has_side_effects=True, vmem_limit_bytes=32 * 1024 * 1024),
        name="modes",
    )(spin_mid, spin_end, jnp.asarray(x_full), jnp.asarray(y_full), jnp.asarray(z_cos.T), jnp.asarray(z_sin.T))
    out = out.reshape(nz, owned, 3, half, 2, 2, KY).transpose(4, 1, 5, 2, 0, 3, 6)
    return out.reshape(2, owned, -1)


def body(polar_angle, azimuth, classes, exchange_table):
    spin_mid, spin_end = evolve(polar_angle, azimuth, classes, exchange_table)
    both = modes(spin_mid, spin_end)
    return (spin_end, both[0], both[1])


def solution(mesh):
    return jax.shard_map(
        body,
        mesh=mesh,
        in_specs=(
            P("gz", ("groups", "gx"), "gy"),
            P("gz", ("groups", "gx"), "gy"),
            P(None, "gz", ("groups", "gx"), "gy"),
            P(),
        ),
        out_specs=(
            P(None, "gz", ("groups", "gx"), "gy"),
            P(("groups", "gx"), None),
            P(("groups", "gx"), None),
        ),
        check_vma=False,
    )
```
